512 devices in a mesh: ctx: 128 (over y, x_hi, z), head: 4 (over x_lo, core).
Axes of the slice: x: 4 (x_hi: 2, x_lo: 2; x = x_hi * 2 + x_lo), y: 8, z: 8, core: 2. Of those that a mesh axis runs over, the one named last changes fastest.
Arguments:
- text_query: bfloat16 [16384, 2560], P('ctx', 'head')
- grad_out: bfloat16 [16384, 2560], P('ctx', 'head'), may hold values from -6 to 6
- frame_kv: bfloat16 [2, 65536, 2560], P(None, 'ctx', 'head')
- sink_logit: float32 [20], P('head'), may hold values from 1 to 6
- pairing: int32 [128], replicated, may hold values from 0 to 127, each once
- block_mask: int32 [128, 4], P('ctx'), may hold values from 0 to 1
- text_seg: int32 [16384], P('ctx'), may hold values from 0 to 3, as said below
- frame_seg: int32 [65536], P('ctx'), may hold values from 0 to 3, as said below
Outputs:
- grad_query: bfloat16 [16384, 2560], P('ctx', 'head')
- grad_kv: bfloat16 [2, 65536, 2560], P(None, ('ctx', 'head'))
The draws below stay inside these ranges and needn't reach their ends.
Inputs may be any that keep to these rules, and one draw needn't show every extreme that they name: pairing is a permutation of the ctx indices. `text_seg`: within the 128 text tokens of each ctx index the ids do not fall and each of the 4 ids appears. `frame_seg`: within the 512 frames of each ctx index the ids do not fall and each of the 4 ids appears.
All inputs are finite; a program needn't handle non-finite values.
Results may differ from the reference program's by a relative error of at most 0.0081.
Values may be sent and summed in bfloat16 or wider, within the bound.
A program may use at most 64 MiB of HBM per device.

```python
import jax
import jax.numpy as jnp
from jax import lax

HEADS = 20
DH = 128
BLOCK = 128
NSEG = 4
TXT = 128
FRM = 512
TEXT = 16384
N_CTX = 128


def draw_text_query(key, part):
    array_shape = (TXT * N_CTX, HEADS * DH)
    result = jnp.clip(jax.random.normal(jax.random.fold_in(key, 1), array_shape, jnp.float32), -6.0, 6.0)
    return result.astype(jnp.bfloat16)


def draw_frame_kv(key, part):
    array_shape = (2, FRM * N_CTX, HEADS * DH)
    result = jnp.clip(jax.random.normal(jax.random.fold_in(key, 2), array_shape, jnp.float32), -6.0, 6.0)
    return result.astype(jnp.bfloat16)


def draw_block_mask(key, part):
    frame_blocks = FRM // BLOCK
    levels = jax.random.randint(jax.random.fold_in(key, 21), (N_CTX,), 1, frame_blocks + 1)
    mark_values = jax.random.randint(jax.random.fold_in(key, 22), (N_CTX, TXT // BLOCK, frame_blocks), 0, frame_blocks)
    result = (mark_values < levels[:, None, None]).astype(jnp.int32)
    return result.reshape(N_CTX * (TXT // BLOCK), frame_blocks)


def segment_ids(key, row_count):
    half_span = row_count // (2 * NSEG)
    offsets = jax.random.randint(key, (N_CTX, NSEG - 1), -half_span, half_span)
    bounds = jnp.arange(1, NSEG, dtype=jnp.int32)[None, :] * (row_count // NSEG) + offsets
    places = jnp.arange(row_count, dtype=jnp.int32)
    result = jnp.sum((places[None, :, None] >= bounds[:, None, :]).astype(jnp.int32), axis=2)
    return result.reshape(N_CTX * row_count).astype(jnp.int32)


def draw_text_seg(key, part):
    return segment_ids(jax.random.fold_in(key, 41), TXT)


def draw_frame_seg(key, part):
    return segment_ids(jax.random.fold_in(key, 42), FRM)


def shard_levels(stream_key, extent, cuts, low, top_value):
    loudness = 1.0
    for position, shards_of in cuts:
        heights = jax.random.uniform(jax.random.fold_in(jax.random.fold_in(stream_key, 6), position), (shards_of,), jnp.float32, low / len(cuts), top_value / len(cuts))
        loudness = loudness * jnp.repeat(jnp.exp(heights), extent[position] // shards_of).reshape((-1,) + (1,) * (len(extent) - 1 - position))
    return loudness


def gaussian(key, shape, width, bound, split=(), kind=jnp.bfloat16):
    array = jax.random.normal(key, shape, jnp.float32) * width
    if len(split) > 0:
        array = shard_levels(key, shape, split, -0.22, 0.18) * array
    return jnp.clip(array, min=-bound, max=bound).astype(kind)


def setup_inputs(seed: int = 0) -> dict:
    key_of = jax.random.split(jax.random.key(seed), 9)
    return {
        "text_query": draw_text_query(jax.random.fold_in(key_of[8], 71), 0),
        "grad_out": gaussian(key_of[1], (TEXT, HEADS * DH), 1.0, 6.0, ((0, 128), (1, 4))),
        "frame_kv": draw_frame_kv(jax.random.fold_in(key_of[8], 71), 0),
        "sink_logit": jnp.clip(1.0 + 5.0 * jax.random.uniform(key_of[3], (HEADS,), jnp.float32) ** shard_levels(key_of[3], (HEADS,), ((0, 4),), -0.2, 0.2), 1.0, 6.0),
        "pairing": jax.random.permutation(key_of[4], N_CTX).astype(jnp.int32),
        "block_mask": draw_block_mask(jax.random.fold_in(key_of[8], 71), 0),
        "text_seg": draw_text_seg(jax.random.fold_in(key_of[8], 71), 0),
        "frame_seg": draw_frame_seg(jax.random.fold_in(key_of[8], 71), 0),
    }


def pair_grads(query_rows, grad_rows, key_rows, value_rows, row_mask, text_ids, frame_ids, sink_logit):
    score_scale = DH ** -0.5
    text_rows = query_rows.shape[0]
    frame_rows = key_rows.shape[0]
    head_count = query_rows.shape[1] // DH
    q_heads = query_rows.reshape(text_rows, head_count, DH).astype(jnp.float32)
    g_heads = grad_rows.reshape(text_rows, head_count, DH).astype(jnp.float32)
    k_heads = key_rows.reshape(frame_rows, head_count, DH).astype(jnp.float32)
    v_heads = value_rows.reshape(frame_rows, head_count, DH).astype(jnp.float32)
    allowed = (jnp.repeat(row_mask, BLOCK, axis=1) == 1) & (text_ids[:, None] == frame_ids[None, :])
    scores = jnp.einsum("the,fhe->htf", q_heads, k_heads) * score_scale
    masked = jnp.where(allowed[None], scores, -1e30)
    row_top = jnp.maximum(sink_logit[:, None], jnp.max(masked, axis=2))
    exp_terms = jnp.where(allowed[None], jnp.exp(masked - row_top[:, :, None]), 0.0)
    row_total = jnp.exp(sink_logit[:, None] - row_top) + jnp.sum(exp_terms, axis=2)
    attention = exp_terms / row_total[:, :, None]
    attention_low = lax.optimization_barrier(attention.astype(jnp.bfloat16)).astype(jnp.float32)
    output = jnp.einsum("htf,fhe->the", attention_low, v_heads)
    grad_attention = jnp.einsum("the,fhe->htf", g_heads, v_heads)
    row_delta = jnp.sum(g_heads * output, axis=2)
    grad_scores = attention * (grad_attention - row_delta.T[:, :, None])
    grad_scores = lax.optimization_barrier(grad_scores.astype(jnp.bfloat16)).astype(jnp.float32)
    grad_query = jnp.einsum("htf,fhe->the", grad_scores, k_heads) * score_scale
    grad_keys = jnp.einsum("htf,the->fhe", grad_scores, q_heads) * score_scale
    grad_values = jnp.einsum("htf,the->fhe", attention_low, g_heads)
    grad_pair = jnp.stack([grad_keys.reshape(frame_rows, -1), grad_values.reshape(frame_rows, -1)])
    return grad_query.reshape(text_rows, -1).astype(jnp.bfloat16), grad_pair.astype(jnp.bfloat16)


def reference(text_query, grad_out, frame_kv, sink_logit, pairing, block_mask, text_seg, frame_seg):
    text_blocks = TXT // BLOCK

    def one_owner(owner_index):
        partner = pairing[owner_index].astype(jnp.int32)
        query_rows = lax.dynamic_slice_in_dim(text_query, owner_index * TXT, TXT, 0)
        grad_rows = lax.dynamic_slice_in_dim(grad_out, owner_index * TXT, TXT, 0)
        key_rows = lax.dynamic_slice_in_dim(frame_kv[0], partner * FRM, FRM, 0)
        value_rows = lax.dynamic_slice_in_dim(frame_kv[1], partner * FRM, FRM, 0)
        mask_rows = lax.dynamic_slice_in_dim(block_mask, owner_index * text_blocks, text_blocks, 0)
        row_mask = jnp.repeat(mask_rows, BLOCK, axis=0)
        text_ids = lax.dynamic_slice_in_dim(text_seg, owner_index * TXT, TXT, 0)
        frame_ids = lax.dynamic_slice_in_dim(frame_seg, partner * FRM, FRM, 0)
        return pair_grads(query_rows, grad_rows, key_rows, value_rows, row_mask, text_ids, frame_ids, sink_logit)

    grad_query, grad_pairs = lax.map(one_owner, jnp.arange(N_CTX, dtype=jnp.int32))
    inverse = jnp.argsort(pairing).astype(jnp.int32)
    grad_owned = jnp.take(grad_pairs, inverse, axis=0)
    grad_kv = jnp.transpose(grad_owned, (1, 0, 2, 3)).reshape(2, N_CTX * FRM, HEADS * DH)
    return grad_query.reshape(N_CTX * TXT, HEADS * DH), grad_kv
```

```python
import functools

import jax
import jax.numpy as jnp
from jax import lax
from jax.experimental import pallas as pl
from jax.experimental.pallas import tpu as pltpu
from jax.sharding import PartitionSpec as P

DH = 128
BLOCK = 128
TILE = 16
GROUPS = ((0, 1), (1, 1), (2, 1), (3, 1), (4, 1))
MESH = pl.DeviceIdType.MESH


def _dot(a, b, ca, cb):
    return lax.dot_general(a, b, (((ca,), (cb,)), ((), ())), preferred_element_type=jnp.float32)


def kernel(
    A, B, H,
    q_hbm, g_hbm, kv_hbm, sink, pair_s, pair_v, mask_v, tseg_v, fseg_v,
    dq_out, dkv_out,
    qg, kv, s1, s2, p3, s3, qr, dkv, dq, r1, r2, rp, r3, tag, ta, tb, fcol, inv_v, inv_s,
    in_sem, inv_sem,
    s1s, s1r, s2s, s2r, s3s, s3r, s4s, s4r,
    ks, kr, r1s, r1r, r2s, r2r, r3s, r3r, r4s, r4r,
    tas, tar, tbs, tbr,
):
    scale = DH ** (-0.5)
    c = lax.axis_index("ctx")
    j = lax.axis_index("head")
    a = c // B
    b = c % B
    core = j % 2
    heads_here = q_hbm.shape[1] // DH
    frames = kv_hbm.shape[1]
    frame_part = frames // H
    n_ctx = A * B

    def on_a(x):
        return {"ctx": x * B + b}

    def on_b(x):
        return {"ctx": a * B + x}

    def member(v):
        v = v % B
        return (v % 2) * (B // 2) + v // 2

    def text_member(i, kind):
        return member(2 * i + kind + 10 * core + 2 * a)

    def grad_member(i):
        return member(3 * i + 8 * core + 2 * a)

    def cols(i):
        first, count = GROUPS[i]
        return slice(first * DH, (first + count) * DH)

    def rows(x):
        return pl.ds(pl.multiple_of(x * TILE, TILE), TILE)

    def send(src, dst, ssem, rsem, where):
        pltpu.make_async_remote_copy(
            src_ref=src, dst_ref=dst, send_sem=ssem, recv_sem=rsem, device_id=where, device_id_type=MESH
        ).start()

    def local(src, dst, sem):
        pltpu.make_async_copy(src, dst, sem).start()

    def wait(ref, sem):
        pltpu.make_async_copy(ref, ref, sem).wait()

    def others(count, me, body):
        def step(k, carry):
            body((me + k) % count)
            return carry

        lax.fori_loop(1, count, step, 0)

    local(q_hbm, qg.at[0], in_sem.at[0])
    local(g_hbm, qg.at[1], in_sem.at[1])
    local(kv_hbm, kv, in_sem.at[2])

    barrier = pltpu.get_barrier_semaphore()

    def greet(where):
        pl.semaphore_signal(barrier, inc=1, device_id=where, device_id_type=MESH)

    others(A, a, lambda x: greet(on_a(x)))
    others(B, b, lambda x: greet(on_b(x)))
    others(H, j, lambda x: greet({"head": x}))

    tag[...] = jnp.zeros(tag.shape, jnp.int32)
    tag[0:1, 0 : tseg_v.shape[1]] = tseg_v[...]
    tag[1:2, 0 : mask_v.shape[1]] = mask_v[...]
    column = jnp.broadcast_to(pair_v[...], (n_ctx, n_ctx)).T
    here = lax.broadcasted_iota(jnp.int32, (n_ctx, n_ctx), 1)
    source = lax.broadcasted_iota(jnp.int32, (n_ctx, n_ctx), 0)
    inv_v[...] = jnp.max(jnp.where(column == here, source, 0), axis=0, keepdims=True)
    local(inv_v, inv_s, inv_sem)

    pl.semaphore_wait(barrier, A + B + H - 3)
    wait(qg.at[0], in_sem.at[0])
    wait(qg.at[1], in_sem.at[1])

    def start_s1(i):
        others(A, a, lambda x: send(qg.at[:, rows(x), cols(i)], s1.at[a, :, :, cols(i)], s1s.at[i], s1r.at[i], on_a(x)))
        local(qg.at[:, rows(a), cols(i)], s1.at[a, :, :, cols(i)], s1r.at[i])

    start_s1(0)
    others(A, a, lambda x: send(tag, ta.at[a], tas, tar, on_a(x)))
    local(tag, ta.at[a], tar)
    for i in range(1, len(GROUPS)):
        start_s1(i)

    for n in range(frames // BLOCK):
        fcol[n * BLOCK : (n + 1) * BLOCK, :] = jnp.broadcast_to(
            fseg_v[n : n + 1, :].astype(jnp.float32), (BLOCK, BLOCK)
        ).T

    def stage_s2(i):
        wait(s1.at[:, :, :, cols(i)], s1r.at[i])
        for kind in range(2):
            to = text_member(i, kind)
            src = s1.at[:, kind, :, cols(i)]
            dst = s2.at[:, b, :, cols(i)]

            @pl.when(to != b)
            def _():
                send(src, dst, s2s.at[i, kind], s2r.at[i], on_b(to))

            @pl.when(to == b)
            def _():
                local(src, dst, s2r.at[i])

        if i == 0:
            wait(ta, tar)
            others(B, b, lambda x: send(ta, tb.at[:, b], tbs, tbr, on_b(x)))
            local(ta, tb.at[:, b], tbr)
            wait(inv_v, inv_sem)

    def place(s):
        return (s // B) & (A - 1), s & (B - 1)

    def reorder(table, i, src, dst):
        def step(n, carry):
            for m in range(A):
                row, col = place(table(m * B + n))
                dst[n, m, :, cols(i)] = src[row, col, :, cols(i)]
            return carry

        lax.fori_loop(0, B, step, 0)

    def stage_s3(i):
        kind = (b == text_member(i, 1)).astype(jnp.int32)

        @pl.when((b == text_member(i, 0)) | (b == text_member(i, 1)))
        def _():
            wait(s2.at[:, :, :, cols(i)], s2r.at[i])
            reorder(lambda n: inv_s[0, n], i, s2, p3)
            others(B, b, lambda x: send(p3.at[x, :, :, cols(i)], s3.at[kind, :, :, cols(i)], s3s.at[i], s3r.at[i], on_b(x)))
            local(p3.at[b, :, :, cols(i)], s3.at[kind, :, :, cols(i)], s3r.at[i])

    def stage_s4(i):
        wait(s3.at[:, :, :, cols(i)], s3r.at[i])
        others(A, a, lambda x: send(s3.at[:, x, :, cols(i)], qr.at[:, rows(a), cols(i)], s4s.at[i], s4r.at[i], on_a(x)))
        local(s3.at[:, a, :, cols(i)], qr.at[:, rows(a), cols(i)], s4r.at[i])

    def attend(h):
        at = slice(h * DH, (h + 1) * DH)
        q = qr[0, :, at]
        g = qr[1, :, at]
        k = kv[0, :, at]
        v = kv[1, :, at]
        row, col = place(inv_s[0, c])
        tags = tb[row, col]
        ids = tags[0:1, 0 : q.shape[0]].astype(jnp.float32)
        scores = _dot(k, q, 1, 1) * scale
        parts = []
        for n in range(frames // BLOCK):
            open_ = jnp.broadcast_to(tags[1:2, n : n + 1], ids.shape) == 1
            wanted = jnp.where(open_, ids, -1.0)
            at_n = slice(n * BLOCK, (n + 1) * BLOCK)
            allowed = fcol[at_n, 0 : q.shape[0]] == wanted
            parts.append(jnp.where(allowed, scores[at_n, :], -1e30))
        masked = jnp.concatenate(parts, axis=0)
        logit = jnp.full((1, q.shape[0]), sink[h], jnp.float32)
        top = jnp.maximum(logit, jnp.max(masked, axis=0, keepdims=True))
        terms = jnp.exp(masked - top)
        total = jnp.exp(logit - top) + jnp.sum(terms, axis=0, keepdims=True)
        attention = terms * (1.0 / total)
        low = attention.astype(jnp.bfloat16)
        grad_attention = _dot(v, g, 1, 1)
        delta = jnp.sum(low.astype(jnp.float32) * grad_attention, axis=0, keepdims=True)
        grad_scores = (attention * (grad_attention - delta)).astype(jnp.bfloat16)
        dq[:, at] = (_dot(grad_scores, k, 0, 0) * scale).astype(jnp.bfloat16)
        dkv[0, :, at] = (_dot(grad_scores, q, 1, 0) * scale).astype(jnp.bfloat16)
        dkv[1, :, at] = _dot(low, g, 1, 0).astype(jnp.bfloat16)

    def stage_compute(i):
        first, count = GROUPS[i]
        if i == 0:
            wait(kv, in_sem.at[2])
            wait(tb, tbr)
        wait(qr.at[:, :, cols(i)], s4r.at[i])
        for h in range(first, first + count):
            attend(h)
        others(A, a, lambda x: send(dq.at[rows(x), cols(i)], r1.at[a, :, cols(i)], r1s.at[i], r1r.at[i], on_a(x)))
        local(dq.at[rows(a), cols(i)], r1.at[a, :, cols(i)], r1r.at[i])
        out_cols = pl.ds(pl.multiple_of((j * heads_here + first) * DH, DH), count * DH)

        def part(x):
            return dkv.at[:, pl.ds(pl.multiple_of(x * frame_part, frame_part), frame_part), cols(i)]

        others(H, j, lambda x: send(part(x), dkv_out.at[:, :, out_cols], ks.at[i], kr.at[i], {"head": x}))
        local(part(j), dkv_out.at[:, :, out_cols], kr.at[i])

    def stage_r2(i):
        wait(r1.at[:, :, cols(i)], r1r.at[i])
        to = grad_member(i)
        src = r1.at[:, :, cols(i)]
        dst = r2.at[:, b, :, cols(i)]

        @pl.when(to != b)
        def _():
            send(src, dst, r2s.at[i], r2r.at[i], on_b(to))

        @pl.when(to == b)
        def _():
            local(src, dst, r2r.at[i])

    def stage_r3(i):
        @pl.when(b == grad_member(i))
        def _():
            wait(r2.at[:, :, :, cols(i)], r2r.at[i])
            reorder(lambda n: pair_s[n], i, r2, rp)
            others(B, b, lambda x: send(rp.at[x, :, :, cols(i)], r3.at[:, :, cols(i)], r3s.at[i], r3r.at[i], on_b(x)))
            local(rp.at[b, :, :, cols(i)], r3.at[:, :, cols(i)], r3r.at[i])

    def stage_r4(i):
        wait(r3.at[:, :, cols(i)], r3r.at[i])
        others(A, a, lambda x: send(r3.at[x, :, cols(i)], dq_out.at[rows(a), cols(i)], r4s.at[i], r4r.at[i], on_a(x)))
        local(r3.at[a, :, cols(i)], dq_out.at[rows(a), cols(i)], r4r.at[i])

    stages = (stage_s2, stage_s3, stage_s4, stage_compute, stage_r2, stage_r3, stage_r4)
    for tick in range(len(GROUPS) + len(stages) - 1):
        for n in reversed(range(len(stages))):
            if 0 <= tick - n < len(GROUPS):
                stages[n](tick - n)

    wait(ta.at[0 : A - 1], tas)
    wait(tb.at[:, 0 : B - 1], tbs)
    for i in range(len(GROUPS)):
        wait(s1.at[0 : A - 1, :, :, cols(i)], s1s.at[i])
        for kind in range(2):

            @pl.when(text_member(i, kind) != b)
            def _():
                wait(s1.at[:, kind, :, cols(i)], s2s.at[i, kind])

        @pl.when((b == text_member(i, 0)) | (b == text_member(i, 1)))
        def _():
            wait(p3.at[0 : B - 1, :, :, cols(i)], s3s.at[i])

        wait(s3.at[:, 0 : A - 1, :, cols(i)], s4s.at[i])
        wait(dkv.at[:, 0 : (H - 1) * frame_part, cols(i)], ks.at[i])
        wait(dkv.at[:, :, cols(i)], kr.at[i])
        wait(r1.at[0 : A - 1, :, cols(i)], r1s.at[i])

        @pl.when(grad_member(i) != b)
        def _():
            wait(r1.at[:, :, cols(i)], r2s.at[i])

        @pl.when(b == grad_member(i))
        def _():
            wait(rp.at[0 : B - 1, :, :, cols(i)], r3s.at[i])

        wait(r3.at[0 : A - 1, :, cols(i)], r4s.at[i])
        wait(dq.at[:, cols(i)], r4r.at[i])


def shards(text_query, grad_out, frame_kv, sink_logit, pairing, block_mask, text_seg, frame_seg):
    n_ctx = lax.axis_size("ctx")
    H = lax.axis_size("head")
    text_rows, width = text_query.shape
    frames = frame_kv.shape[1]
    A = text_rows // TILE
    B = n_ctx // A
    n = len(GROUPS)
    bf = jnp.bfloat16
    dma = pltpu.SemaphoreType.DMA
    anywhere = pl.BlockSpec(memory_space=pl.ANY)
    vmem = pl.BlockSpec(memory_space=pltpu.VMEM)
    smem = pl.BlockSpec(memory_space=pltpu.SMEM)
    return pl.pallas_call(
        functools.partial(kernel, A, B, H),
        out_shape=(
            jax.ShapeDtypeStruct((text_rows, width), bf),
            jax.ShapeDtypeStruct((2, frames // H, width * H), bf),
        ),
        in_specs=[anywhere, anywhere, anywhere, smem, smem, vmem, vmem, vmem, vmem],
        out_specs=(anywhere, anywhere),
        scratch_shapes=[
            pltpu.VMEM((2, text_rows, width), bf),
            pltpu.VMEM((2, frames, width), bf),
            pltpu.VMEM((A, 2, TILE, width), bf),
            pltpu.VMEM((A, B, TILE, width), bf),
            pltpu.VMEM((B, A, TILE, width), bf),
            pltpu.VMEM((2, A, TILE, width), bf),
            pltpu.VMEM((2, text_rows, width), bf),
            pltpu.VMEM((2, frames, width), bf),
            pltpu.VMEM((text_rows, width), bf),
            pltpu.VMEM((A, TILE, width), bf),
            pltpu.VMEM((A, B, TILE, width), bf),
            pltpu.VMEM((B, A, TILE, width), bf),
            pltpu.VMEM((A, TILE, width), bf),
            pltpu.VMEM((2, 128), jnp.int32),
            pltpu.VMEM((A, 2, 128), jnp.int32),
            pltpu.VMEM((A, B, 2, 128), jnp.int32),
            pltpu.VMEM((frames, BLOCK), jnp.float32),
            pltpu.VMEM((1, n_ctx), jnp.int32),
            pltpu.SMEM((1, n_ctx), jnp.int32),
            dma((3,)),
            dma,
            dma((n,)), dma((n,)), dma((n, 2)), dma((n,)), dma((n,)), dma((n,)), dma((n,)), dma((n,)),
            dma((n,)), dma((n,)), dma((n,)), dma((n,)), dma((n,)), dma((n,)), dma((n,)), dma((n,)), dma((n,)), dma((n,)),
            dma, dma, dma, dma,
        ],
        compiler_params=pltpu.CompilerParams(
            collective_id=0, has_side_effects=True, vmem_limit_bytes=40 * 1024 * 1024
        ),
        name="paired_attention_grads",
    )(
        text_query,
        grad_out,
        frame_kv,
        sink_logit,
        pairing,
        pairing.reshape(1, n_ctx),
        block_mask,
        text_seg.reshape(1, text_rows),
        frame_seg.reshape(frames // BLOCK, BLOCK),
    )


def solution(mesh):
    in_specs = (
        P("ctx", "head"),
        P("ctx", "head"),
        P(None, "ctx", "head"),
        P("head"),
        P(),
        P("ctx", None),
        P("ctx"),
        P("ctx"),
    )
    out_specs = (P("ctx", "head"), P(None, ("ctx", "head"), None))
    return jax.shard_map(shards, mesh=mesh, in_specs=in_specs, out_specs=out_specs, check_vma=False)
```

```python
import functools

import jax
import jax.numpy as jnp
from jax import lax
from jax.experimental import pallas as pl
from jax.experimental.pallas import tpu as pltpu
from jax.sharding import PartitionSpec as P

DH = 128
BLOCK = 128
TILE = 16
MESH = pl.DeviceIdType.MESH


def _dot(a, b, ca, cb):
    return lax.dot_general(a, b, (((ca,), (cb,)), ((), ())), preferred_element_type=jnp.float32)


def kernel(
    N, H,
    q_hbm, g_hbm, kv_hbm, sink_hbm, pair_hbm, mask_hbm, tseg_hbm, fseg_hbm,
    dq_out, dkv_out,
    qg, kv, arrived, ordered, qr, dkv, dq, tag, tags_in, tags_out, tag_here,
    fcol, sink, pair_s, pair_v, mask_v, tseg_v, fseg_v, inv_v, inv_s,
    in_sem, inv_sem,
    t1s, t1r, t2s, t2r, g1s, g1r, g2s, g2r, ks, kr, a1s, a1r, a2s, a2r,
):
    scale = DH ** (-0.5)
    c = lax.axis_index("ctx")
    j = lax.axis_index("head")
    text_rows = q_hbm.shape[0]
    heads_here = q_hbm.shape[1] // DH
    frames = kv_hbm.shape[1]
    frame_part = frames // H
    blocks = text_rows // TILE
    pieces = 2 * blocks
    text_roles = heads_here * pieces
    grad_roles = heads_here * blocks
    tag_role = text_roles + grad_roles
    core = j % 2

    def member(role):
        if N != 128:
            return jnp.where(core == 1, N - 1 - role, role)
        y, x, r = role & 7, (role >> 3) & 1, role >> 4
        r = jnp.where(core == 1, 7 - r, r)
        turned = ((r & 1) << 2) | (r & 2) | (r >> 2)
        return (y << 4) | (x << 3) | ((3 * y + 4 * x + turned) & 7)

    def role_of(device):
        if N != 128:
            return jnp.where(core == 1, N - 1 - device, device)
        y, x, z = device >> 4, (device >> 3) & 1, device & 7
        turned = (z + 32 - 3 * y - 4 * x) & 7
        r = ((turned & 1) << 2) | (turned & 2) | (turned >> 2)
        r = jnp.where(core == 1, 7 - r, r)
        return (r << 4) | (x << 3) | y

    role = role_of(c)
    is_text = role < text_roles
    is_grad = (role >= text_roles) & (role < tag_role)
    is_tag = role == tag_role

    def cols(h):
        return pl.ds(pl.multiple_of(h * DH, DH), DH)

    def rows(x):
        return pl.ds(pl.multiple_of(x * TILE, TILE), TILE)

    def send(src, dst, ssem, rsem, ctx):
        pltpu.make_async_remote_copy(
            src_ref=src, dst_ref=dst, send_sem=ssem, recv_sem=rsem, device_id={"ctx": ctx}, device_id_type=MESH
        ).start()

    def local(src, dst, sem):
        pltpu.make_async_copy(src, dst, sem).start()

    def wait(ref, sem):
        pltpu.make_async_copy(ref, ref, sem).wait()

    def loop(low, high, body):
        def step(k, carry):
            body(k)
            return carry

        lax.fori_loop(low, high, step, 0)

    def send_or_keep(src, dst, ssem, rsem, to):
        @pl.when(to != c)
        def _():
            send(src, dst, ssem, rsem, to)

        @pl.when(to == c)
        def _():
            local(src, dst, rsem)

    barrier = pltpu.get_barrier_semaphore()
    loop(1, N, lambda k: pl.semaphore_signal(barrier, inc=1, device_id={"ctx": (c + k) % N}, device_id_type=MESH))
    loop(1, H, lambda k: pl.semaphore_signal(barrier, inc=1, device_id={"head": (j + k) % H}, device_id_type=MESH))

    local(mask_hbm, mask_v, in_sem.at[3])
    local(tseg_hbm, tseg_v, in_sem.at[4])
    local(pair_hbm, pair_v, in_sem.at[5])
    local(q_hbm, qg.at[0], in_sem.at[0])
    local(g_hbm, qg.at[1], in_sem.at[1])
    local(pair_hbm, pair_s, in_sem.at[6])
    local(sink_hbm, sink, in_sem.at[7])
    local(fseg_hbm, fseg_v, in_sem.at[8])
    local(kv_hbm, kv, in_sem.at[2])

    tag[...] = jnp.zeros(tag.shape, jnp.int32)
    wait(mask_v, in_sem.at[3])
    wait(tseg_v, in_sem.at[4])
    wait(pair_v, in_sem.at[5])
    tag[0:1, 0:text_rows] = tseg_v[...]
    tag[1:2, 0 : mask_v.shape[1]] = mask_v[...]
    column = jnp.broadcast_to(pair_v[...], (N, N)).T
    here = lax.broadcasted_iota(jnp.int32, (N, N), 1)
    source = lax.broadcasted_iota(jnp.int32, (N, N), 0)
    inv_v[...] = jnp.max(jnp.where(column == here, source, 0), axis=0, keepdims=True)
    local(inv_v, inv_s, inv_sem)
    wait(fseg_v, in_sem.at[8])
    for n in range(frames // BLOCK):
        fcol[n * BLOCK : (n + 1) * BLOCK, :] = jnp.broadcast_to(
            fseg_v[n : n + 1, :].astype(jnp.float32), (BLOCK, BLOCK)
        ).T
    wait(inv_v, inv_sem)
    wait(pair_s, in_sem.at[6])
    wait(sink, in_sem.at[7])
    wait(qg.at[0], in_sem.at[0])
    wait(qg.at[1], in_sem.at[1])
    wait(kv, in_sem.at[2])
    pl.semaphore_wait(barrier, N + H - 2)

    send_or_keep(tag, tags_in.at[c], a1s, a1r, member(jnp.int32(tag_role)))
    for h in range(heads_here):

        def to_member(k):
            piece = (k + c) % pieces
            src = qg.at[piece // blocks, rows(piece % blocks), cols(h)]
            send_or_keep(src, arrived.at[c], t1s, t1r, member(h * pieces + piece))

        loop(0, pieces, to_member)

    def place(s):
        return s & (N - 1)

    def pass_on(table, src, dst, target, ssem, rsem):
        def step(n, carry):
            for m in range(8):
                to = (c + n * 8 + m) % N
                dst[to] = src[place(table[0, to])]
            for m in range(8):
                to = (c + n * 8 + m) % N
                send_or_keep(dst.at[to], target, ssem, rsem, to)
            return carry

        lax.fori_loop(0, N // 8, step, 0)

    @pl.when(is_tag)
    def _():
        wait(tags_in, a1r)
        pass_on(inv_s, tags_in, tags_out, tag_here, a2s, a2r)

    @pl.when(is_text)
    def _():
        head, piece = role // pieces, role % pieces
        wait(arrived, t1r)
        pass_on(inv_s, arrived, ordered, qr.at[piece // blocks, rows(piece % blocks), cols(head)], t2s, t2r.at[head])

    wait(tag_here, a2r)

    def attend(h):
        at = slice(h * DH, (h + 1) * DH)
        q = qr[0, :, at]
        g = qr[1, :, at]
        k = kv[0, :, at]
        v = kv[1, :, at]
        ids = tag_here[0:1, 0:text_rows].astype(jnp.float32)
        scores = _dot(k, q, 1, 1) * scale
        parts = []
        for n in range(frames // BLOCK):
            open_ = jnp.broadcast_to(tag_here[1:2, n : n + 1], ids.shape) == 1
            wanted = jnp.where(open_, ids, -1.0)
            at_n = slice(n * BLOCK, (n + 1) * BLOCK)
            allowed = fcol[at_n, 0:text_rows] == wanted
            parts.append(jnp.where(allowed, scores[at_n, :], -1e30))
        masked = jnp.concatenate(parts, axis=0)
        logit = jnp.full((1, text_rows), sink[0, h], jnp.float32)
        top = jnp.maximum(logit, jnp.max(masked, axis=0, keepdims=True))
        terms = jnp.exp(masked - top)
        total = jnp.exp(logit - top) + jnp.sum(terms, axis=0, keepdims=True)
        attention = terms * (1.0 / total)
        low = attention.astype(jnp.bfloat16)
        grad_attention = _dot(v, g, 1, 1)
        delta = jnp.sum(low.astype(jnp.float32) * grad_attention, axis=0, keepdims=True)
        grad_scores = (attention * (grad_attention - delta)).astype(jnp.bfloat16)
        dq[:, at] = (_dot(grad_scores, k, 0, 0) * scale).astype(jnp.bfloat16)

        def to_grad_member(n):
            block = (n + c) % blocks
            send_or_keep(
                dq.at[rows(block), at], arrived_grad.at[c], g1s, g1r, member(text_roles + h * blocks + block)
            )

        loop(0, blocks, to_grad_member)
        dkv[0, :, at] = (_dot(grad_scores, q, 1, 0) * scale).astype(jnp.bfloat16)
        dkv[1, :, at] = _dot(low, g, 1, 0).astype(jnp.bfloat16)
        out_cols = pl.ds(pl.multiple_of((j * heads_here + h) * DH, DH), DH)

        def part(x):
            return dkv.at[:, pl.ds(pl.multiple_of(x * frame_part, frame_part), frame_part), at]

        def to_peer(n):
            x = (j + n) % H
            pltpu.make_async_remote_copy(
                src_ref=part(x),
                dst_ref=dkv_out.at[:, :, out_cols],
                send_sem=ks,
                recv_sem=kr,
                device_id={"head": x},
                device_id_type=MESH,
            ).start()

        loop(1, H, to_peer)
        local(part(j), dkv_out.at[:, :, out_cols], kr)

    arrived_grad = arrived
    for h in range(heads_here):
        wait(qr.at[:, :, h * DH : (h + 1) * DH], t2r.at[h])
        attend(h)

    @pl.when(is_grad)
    def _():
        mine = role - text_roles
        wait(arrived, g1r)
        pass_on(pair_s, arrived, ordered, dq_out.at[rows(mine % blocks), cols(mine // blocks)], g2s, g2r)

    wait(dq, g2r)
    wait(dkv, kr)
    wait(dkv.at[:, 0 : (H - 1) * frame_part, :], ks)

    def sent(count, own, ssem):
        @pl.when(own)
        def _():
            wait(arrived.at[0 : count - 1], ssem)

        @pl.when(jnp.logical_not(own))
        def _():
            wait(arrived.at[0:count], ssem)

    sent(text_roles, is_text, t1s)
    sent(grad_roles, is_grad, g1s)

    @pl.when(jnp.logical_not(is_tag))
    def _():
        wait(tag, a1s)

    @pl.when(is_tag)
    def _():
        wait(tags_out.at[0 : N - 1], a2s)

    @pl.when(is_text)
    def _():
        wait(ordered.at[0 : N - 1], t2s)

    @pl.when(is_grad)
    def _():
        wait(ordered.at[0 : N - 1], g2s)


def shards(text_query, grad_out, frame_kv, sink_logit, pairing, block_mask, text_seg, frame_seg):
    N = lax.axis_size("ctx")
    H = lax.axis_size("head")
    text_rows, width = text_query.shape
    frames = frame_kv.shape[1]
    bf = jnp.bfloat16
    dma = pltpu.SemaphoreType.DMA
    hbm = pl.BlockSpec(memory_space=pltpu.HBM)
    return pl.pallas_call(
        functools.partial(kernel, N, H),
        out_shape=(
            jax.ShapeDtypeStruct((text_rows, width), bf),
            jax.ShapeDtypeStruct((2, frames // H, width * H), bf),
        ),
        in_specs=[hbm] * 8,
        out_specs=(hbm, hbm),
        scratch_shapes=[
            pltpu.VMEM((2, text_rows, width), bf),
            pltpu.VMEM((2, frames, width), bf),
            pltpu.VMEM((N, TILE, DH), bf),
            pltpu.VMEM((N, TILE, DH), bf),
            pltpu.VMEM((2, text_rows, width), bf),
            pltpu.VMEM((2, frames, width), bf),
            pltpu.VMEM((text_rows, width), bf),
            pltpu.VMEM((2, 128), jnp.int32),
            pltpu.VMEM((N, 2, 128), jnp.int32),
            pltpu.VMEM((N, 2, 128), jnp.int32),
            pltpu.VMEM((2, 128), jnp.int32),
            pltpu.VMEM((frames, BLOCK), jnp.float32),
            pltpu.SMEM((1, width // DH), jnp.float32),
            pltpu.SMEM((1, N), jnp.int32),
            pltpu.VMEM((1, N), jnp.int32),
            pltpu.VMEM((1, frames // BLOCK), jnp.int32),
            pltpu.VMEM((1, text_rows), jnp.int32),
            pltpu.VMEM((frames // BLOCK, BLOCK), jnp.int32),
            pltpu.VMEM((1, N), jnp.int32),
            pltpu.SMEM((1, N), jnp.int32),
            dma((9,)),
            dma,
            dma, dma, dma, dma((width // DH,)), dma, dma, dma, dma, dma, dma, dma, dma, dma, dma,
        ],
        compiler_params=pltpu.CompilerParams(
            collective_id=0, has_side_effects=True, vmem_limit_bytes=62 * 1024 * 1024
        ),
        name="paired_attention_grads",
    )(
        text_query,
        grad_out,
        frame_kv,
        sink_logit.reshape(1, width // DH),
        pairing.reshape(1, N),
        block_mask,
        text_seg.reshape(1, text_rows),
        frame_seg.reshape(frames // BLOCK, BLOCK),
    )


def solution(mesh):
    in_specs = (
        P("ctx", "head"),
        P("ctx", "head"),
        P(None, "ctx", "head"),
        P("head"),
        P(),
        P("ctx", None),
        P("ctx"),
        P("ctx"),
    )
    out_specs = (P("ctx", "head"), P(None, ("ctx", "head"), None))
    return jax.shard_map(shards, mesh=mesh, in_specs=in_specs, out_specs=out_specs, check_vma=False)
```

```python
import functools

import jax
import jax.numpy as jnp
from jax import lax
from jax.experimental import pallas as pl
from jax.experimental.pallas import tpu as pltpu
from jax.sharding import PartitionSpec as P

DH = 128
BLOCK = 128
TILE = 8
MESH = pl.DeviceIdType.MESH


def _dot(a, b, ca, cb):
    return lax.dot_general(a, b, (((ca,), (cb,)), ((), ())), preferred_element_type=jnp.float32)


def kernel(
    N, H,
    q_hbm, g_hbm, kv_hbm, sink_hbm, pair_hbm, mask_hbm, tseg_hbm, fseg_hbm,
    dq_out, dkv_out,
    qg, kv, arrived, ordered, arrived_more, ordered_more, arrived_grad, ordered_grad, qr, dkv, dq, tag, tags_in, tags_out, tag_here,
    fcol, sink, pair_s, pair_v, mask_v, tseg_v, fseg_v, inv_v, inv_s,
    in_sem, inv_sem,
    t1s, t1r, t2s, t2r, m1r, m2s, g1s, g1r, g2s, g2r, ks, kr, a1s, a1r, a2s, a2r,
):
    scale = DH ** (-0.5)
    c = lax.axis_index("ctx")
    j = lax.axis_index("head")
    text_rows = q_hbm.shape[0]
    heads_here = q_hbm.shape[1] // DH
    frames = kv_hbm.shape[1]
    frame_part = frames // H
    blocks = text_rows // TILE
    pieces = 2 * blocks
    text_roles = heads_here * pieces
    grad_roles = heads_here * blocks
    more = max(text_roles - N, 0)
    first_grad = N - grad_roles
    tag_role = N // 4
    core = j % 2 if N == 128 else 0
    partner = (j + H // 2) % H

    def member(role):
        if N != 128:
            return jnp.where(core == 1, N - 1 - role, role)
        y, x, r = role & 7, (role >> 3) & 1, role >> 4
        r = jnp.where(core == 1, 7 - r, r)
        turned = ((r & 1) << 2) | (r & 2) | (r >> 2)
        return (y << 4) | (x << 3) | ((3 * y + 4 * x + turned) & 7)

    def role_of(device):
        if N != 128:
            return jnp.where(core == 1, N - 1 - device, device)
        y, x, z = device >> 4, (device >> 3) & 1, device & 7
        turned = (z + 32 - 3 * y - 4 * x) & 7
        r = ((turned & 1) << 2) | (turned & 2) | (turned >> 2)
        r = jnp.where(core == 1, 7 - r, r)
        return (r << 4) | (x << 3) | y

    role = role_of(c)
    is_text = role < text_roles
    is_grad = role >= first_grad
    is_tag = role == tag_role
    is_more = role < more

    def cols(h):
        return pl.ds(pl.multiple_of(h * DH, DH), DH)

    def rows(x):
        return pl.ds(pl.multiple_of(x * TILE, TILE), TILE)

    def send(src, dst, ssem, rsem, ctx):
        pltpu.make_async_remote_copy(
            src_ref=src, dst_ref=dst, send_sem=ssem, recv_sem=rsem, device_id=(ctx, partner), device_id_type=MESH
        ).start()

    def local(src, dst, sem):
        pltpu.make_async_copy(src, dst, sem).start()

    def wait(ref, sem):
        pltpu.make_async_copy(ref, ref, sem).wait()

    def loop(low, high, body):
        def step(k, carry):
            body(k)
            return carry

        lax.fori_loop(low, high, step, 0)

    barrier = pltpu.get_barrier_semaphore()
    loop(0, N, lambda k: pl.semaphore_signal(barrier, inc=1, device_id=((c + 37 * k) % N, partner), device_id_type=MESH))
    loop(1, H, lambda k: pl.semaphore_signal(barrier, inc=1, device_id={"head": (j + k) % H}, device_id_type=MESH))

    local(mask_hbm, mask_v, in_sem.at[3])
    local(tseg_hbm, tseg_v, in_sem.at[4])
    local(pair_hbm, pair_v, in_sem.at[5])
    local(q_hbm, qg.at[0], in_sem.at[0])
    local(g_hbm, qg.at[1], in_sem.at[1])
    local(pair_hbm, pair_s, in_sem.at[6])
    local(sink_hbm, sink, in_sem.at[7])
    local(fseg_hbm, fseg_v, in_sem.at[8])
    local(kv_hbm, kv, in_sem.at[2])

    tag[...] = jnp.zeros(tag.shape, jnp.int32)
    wait(mask_v, in_sem.at[3])
    wait(tseg_v, in_sem.at[4])
    wait(pair_v, in_sem.at[5])
    tag[0:1, 0:text_rows] = tseg_v[...]
    tag[1:2, 0 : mask_v.shape[1]] = mask_v[...]
    column = jnp.broadcast_to(pair_v[...], (N, N)).T
    here = lax.broadcasted_iota(jnp.int32, (N, N), 1)
    source = lax.broadcasted_iota(jnp.int32, (N, N), 0)
    inv_v[...] = jnp.max(jnp.where(column == here, source, 0), axis=0, keepdims=True)
    local(inv_v, inv_s, inv_sem)
    wait(fseg_v, in_sem.at[8])
    for n in range(frames // BLOCK):
        fcol[n * BLOCK : (n + 1) * BLOCK, :] = jnp.broadcast_to(
            fseg_v[n : n + 1, :].astype(jnp.float32), (BLOCK, BLOCK)
        ).T
    wait(inv_v, inv_sem)
    wait(pair_s, in_sem.at[6])
    wait(sink, in_sem.at[7])
    wait(qg.at[0], in_sem.at[0])
    wait(qg.at[1], in_sem.at[1])
    wait(kv, in_sem.at[2])
    pl.semaphore_wait(barrier, N + H - 1)

    send(tag, tags_in.at[c], a1s, a1r, member(jnp.int32(tag_role)))
    for h in range(heads_here):

        def to_member(k):
            piece = (k + c) % pieces
            slot = h * pieces + piece
            src = qg.at[piece // blocks, rows(piece % blocks), cols(h)]
            if (h + 1) * pieces <= N:
                send(src, arrived.at[c], t1s, t1r, member(slot))
            elif h * pieces >= N:
                send(src, arrived_more.at[c], t1s, m1r, member(slot - N))
            else:

                @pl.when(slot < N)
                def _():
                    send(src, arrived.at[c], t1s, t1r, member(slot))

                @pl.when(slot >= N)
                def _():
                    send(src, arrived_more.at[c], t1s, m1r, member(slot - N))

        loop(0, pieces, to_member)

    def place(s):
        return s & (N - 1)

    def pass_on(table, src, dst, target, ssem, rsem):
        def step(n, carry):
            for m in range(8):
                to = (c + 37 * (n * 8 + m)) % N
                dst[to] = src[place(table[0, to])]
            for m in range(8):
                to = (c + 37 * (n * 8 + m)) % N
                send(dst.at[to], target, ssem, rsem, to)
            return carry

        lax.fori_loop(0, N // 8, step, 0)

    @pl.when(is_tag)
    def _():
        wait(tags_in, a1r)
        pass_on(inv_s, tags_in, tags_out, tag_here, a2s, a2r)

    def text_pass(slot, src, dst, rsem, ssem):
        head, piece = slot // pieces, slot % pieces
        wait(src, rsem)
        target = qr.at[piece // blocks, rows(piece % blocks), cols(head)]
        pass_on(inv_s, src, dst, target, ssem, t2r.at[head])

    @pl.when(is_text)
    def _():
        text_pass(role, arrived, ordered, t1r, t2s)

    if more:

        @pl.when(is_more)
        def _():
            text_pass(role + N, arrived_more, ordered_more, m1r, m2s)

    wait(tag_here, a2r)

    def attend(h):
        at = slice(h * DH, (h + 1) * DH)
        q = qr[0, :, at]
        g = qr[1, :, at]
        k = kv[0, :, at]
        v = kv[1, :, at]
        ids = tag_here[0:1, 0:text_rows].astype(jnp.float32)
        scores = _dot(k, q, 1, 1) * scale
        parts = []
        for n in range(frames // BLOCK):
            open_ = jnp.broadcast_to(tag_here[1:2, n : n + 1], ids.shape) == 1
            wanted = jnp.where(open_, ids, -1.0)
            at_n = slice(n * BLOCK, (n + 1) * BLOCK)
            allowed = fcol[at_n, 0:text_rows] == wanted
            parts.append(jnp.where(allowed, scores[at_n, :], -1e30))
        masked = jnp.concatenate(parts, axis=0)
        logit = jnp.full((1, text_rows), sink[0, h], jnp.float32)
        top = jnp.maximum(logit, jnp.max(masked, axis=0, keepdims=True))
        terms = jnp.exp(masked - top)
        total = jnp.exp(logit - top) + jnp.sum(terms, axis=0, keepdims=True)
        attention = terms * (1.0 / total)
        low = attention.astype(jnp.bfloat16)
        grad_attention = _dot(v, g, 1, 1)
        delta = jnp.sum(low.astype(jnp.float32) * grad_attention, axis=0, keepdims=True)
        grad_scores = (attention * (grad_attention - delta)).astype(jnp.bfloat16)
        dq[:, at] = (_dot(grad_scores, k, 0, 0) * scale).astype(jnp.bfloat16)

        def to_grad_member(n):
            block = (n + c) % blocks
            send(
                dq.at[rows(block), at], arrived_grad.at[c], g1s, g1r, member(first_grad + h * blocks + block)
            )

        loop(0, blocks, to_grad_member)
        dkv[0, :, at] = (_dot(grad_scores, q, 1, 0) * scale).astype(jnp.bfloat16)
        dkv[1, :, at] = _dot(low, g, 1, 0).astype(jnp.bfloat16)
        out_cols = pl.ds(pl.multiple_of((j * heads_here + h) * DH, DH), DH)

        def part(x):
            return dkv.at[:, pl.ds(pl.multiple_of(x * frame_part, frame_part), frame_part), at]

        def to_peer(n):
            x = (j + n) % H
            pltpu.make_async_remote_copy(
                src_ref=part(x),
                dst_ref=dkv_out.at[:, :, out_cols],
                send_sem=ks,
                recv_sem=kr,
                device_id={"head": x},
                device_id_type=MESH,
            ).start()

        loop(1, H, to_peer)
        local(part(j), dkv_out.at[:, :, out_cols], kr)

    for h in range(heads_here):
        wait(qr.at[:, :, h * DH : (h + 1) * DH], t2r.at[h])
        attend(h)

    @pl.when(is_grad)
    def _():
        mine = role - first_grad
        wait(arrived_grad, g1r)
        pass_on(pair_s, arrived_grad, ordered_grad, dq_out.at[rows(mine % blocks), cols(mine // blocks)], g2s, g2r)

    wait(dq, g2r)
    wait(dkv, kr)
    wait(dkv.at[:, 0 : (H - 1) * frame_part, :], ks)

    wait(qg, t1s)
    wait(dq, g1s)
    wait(tag, a1s)

    @pl.when(is_tag)
    def _():
        wait(tags_out, a2s)

    @pl.when(is_text)
    def _():
        wait(ordered, t2s)

    if more:

        @pl.when(is_more)
        def _():
            wait(ordered_more, m2s)

    @pl.when(is_grad)
    def _():
        wait(ordered_grad, g2s)


def shards(text_query, grad_out, frame_kv, sink_logit, pairing, block_mask, text_seg, frame_seg):
    N = lax.axis_size("ctx")
    H = lax.axis_size("head")
    text_rows, width = text_query.shape
    frames = frame_kv.shape[1]
    bf = jnp.bfloat16
    dma = pltpu.SemaphoreType.DMA
    hbm = pl.BlockSpec(memory_space=pltpu.HBM)
    return pl.pallas_call(
        functools.partial(kernel, N, H),
        out_shape=(
            jax.ShapeDtypeStruct((text_rows, width), bf),
            jax.ShapeDtypeStruct((2, frames // H, width * H), bf),
        ),
        in_specs=[hbm] * 8,
        out_specs=(hbm, hbm),
        scratch_shapes=[
            pltpu.VMEM((2, text_rows, width), bf),
            pltpu.VMEM((2, frames, width), bf),
            pltpu.VMEM((N, TILE, DH), bf),
            pltpu.VMEM((N, TILE, DH), bf),
            pltpu.VMEM((N, TILE, DH), bf),
            pltpu.VMEM((N, TILE, DH), bf),
            pltpu.VMEM((N, TILE, DH), bf),
            pltpu.VMEM((N, TILE, DH), bf),
            pltpu.VMEM((2, text_rows, width), bf),
            pltpu.VMEM((2, frames, width), bf),
            pltpu.VMEM((text_rows, width), bf),
            pltpu.VMEM((2, 128), jnp.int32),
            pltpu.VMEM((N, 2, 128), jnp.int32),
            pltpu.VMEM((N, 2, 128), jnp.int32),
            pltpu.VMEM((2, 128), jnp.int32),
            pltpu.VMEM((frames, BLOCK), jnp.float32),
            pltpu.SMEM((1, width // DH), jnp.float32),
            pltpu.SMEM((1, N), jnp.int32),
            pltpu.VMEM((1, N), jnp.int32),
            pltpu.VMEM((1, frames // BLOCK), jnp.int32),
            pltpu.VMEM((1, text_rows), jnp.int32),
            pltpu.VMEM((frames // BLOCK, BLOCK), jnp.int32),
            pltpu.VMEM((1, N), jnp.int32),
            pltpu.SMEM((1, N), jnp.int32),
            dma((9,)),
            dma,
            dma, dma, dma, dma((width // DH,)), dma, dma, dma, dma, dma, dma, dma, dma, dma, dma, dma, dma,
        ],
        compiler_params=pltpu.CompilerParams(
            collective_id=0, has_side_effects=True, vmem_limit_bytes=40 * 1024 * 1024
        ),
        name="paired_attention_grads",
    )(
        *(
            pltpu.with_memory_space_constraint(x, pltpu.HBM)
            for x in (
                text_query,
                grad_out,
                frame_kv,
                sink_logit.reshape(1, width // DH),
                pairing.reshape(1, N),
                block_mask,
                text_seg.reshape(1, text_rows),
                frame_seg.reshape(frames // BLOCK, BLOCK),
            )
        )
    )


def solution(mesh):
    in_specs = (
        P("ctx", "head"),
        P("ctx", "head"),
        P(None, "ctx", "head"),
        P("head"),
        P(),
        P("ctx", None),
        P("ctx"),
        P("ctx"),
    )
    out_specs = (P("ctx", "head"), P(None, ("ctx", "head"), None))
    return jax.shard_map(shards, mesh=mesh, in_specs=in_specs, out_specs=out_specs, check_vma=False)
```

```python
import functools

import jax
import jax.numpy as jnp
from jax import lax
from jax.experimental import pallas as pl
from jax.experimental.pallas import tpu as pltpu
from jax.sharding import PartitionSpec as P

DH = 128
BLOCK = 128
TILE = 8
MESH = pl.DeviceIdType.MESH


def _dot(a, b, ca, cb):
    return lax.dot_general(a, b, (((ca,), (cb,)), ((), ())), preferred_element_type=jnp.float32)


def kernel(
    N, H,
    q_hbm, g_hbm, kv_hbm, sink_hbm, pair_hbm, mask_hbm, tseg_hbm, fseg_hbm,
    dq_out, dkv_out,
    qg, kv, arrived, ordered, arrived_more, ordered_more, arrived_grad, ordered_grad, qr, dkv, dq, tag, tags_in, tags_out, tag_here,
    low_kept, scores_kept, fcol, sink, pair_s, pair_v, mask_v, tseg_v, fseg_v, inv_v, inv_s,
    in_sem, inv_sem,
    t1s, t1r, t2s, t2r, m1r, m2s, g1s, g1r, g2s, g2r, ks, kr, a1s, a1r, a2s, a2r,
):
    scale = DH ** (-0.5)
    c = lax.axis_index("ctx")
    j = lax.axis_index("head")
    text_rows = q_hbm.shape[0]
    heads_here = q_hbm.shape[1] // DH
    frames = kv_hbm.shape[1]
    frame_part = frames // H
    blocks = text_rows // TILE
    pieces = 2 * blocks
    text_roles = heads_here * pieces
    grad_roles = heads_here * blocks
    more = max(text_roles - N, 0)
    first_grad = N - grad_roles
    tag_role = N // 4
    core = j % 2 if N == 128 else 0
    partner = (j + H // 2) % H

    def member(role):
        if N != 128:
            return jnp.where(core == 1, N - 1 - role, role)
        y, x, r = role & 7, (role >> 3) & 1, role >> 4
        r = jnp.where(core == 1, 7 - r, r)
        turned = ((r & 1) << 2) | (r & 2) | (r >> 2)
        return (y << 4) | (x << 3) | ((3 * y + 4 * x + turned) & 7)

    def role_of(device):
        if N != 128:
            return jnp.where(core == 1, N - 1 - device, device)
        y, x, z = device >> 4, (device >> 3) & 1, device & 7
        turned = (z + 32 - 3 * y - 4 * x) & 7
        r = ((turned & 1) << 2) | (turned & 2) | (turned >> 2)
        r = jnp.where(core == 1, 7 - r, r)
        return (r << 4) | (x << 3) | y

    role = role_of(c)
    is_text = role < text_roles
    is_grad = role >= first_grad
    is_tag = role == tag_role
    is_more = role < more

    outer = 8 if N == 128 else 1

    def far(i):
        return 4 + (1 - 2 * (i % 2)) * ((i + 1) // 2)

    def target_of(i, m):
        if N != 128:
            return (c + m) % N
        y, x, z = c >> 4, (c >> 3) & 1, c & 7
        return (((y + far(m // 2)) & 7) << 4) | (((x + m % 2) & 1) << 3) | ((z + far(i)) & 7)

    def cols(h):
        return pl.ds(pl.multiple_of(h * DH, DH), DH)

    def rows(x):
        return pl.ds(pl.multiple_of(x * TILE, TILE), TILE)

    def send(src, dst, ssem, rsem, ctx):
        pltpu.make_async_remote_copy(
            src_ref=src, dst_ref=dst, send_sem=ssem, recv_sem=rsem, device_id=(ctx, partner), device_id_type=MESH
        ).start()

    def local(src, dst, sem):
        pltpu.make_async_copy(src, dst, sem).start()

    def wait(ref, sem):
        pltpu.make_async_copy(ref, ref, sem).wait()

    def loop(low, high, body):
        def step(k, carry):
            body(k)
            return carry

        lax.fori_loop(low, high, step, 0)

    barrier = pltpu.get_barrier_semaphore()

    def greet(i):
        for m in range(N // outer):
            pl.semaphore_signal(barrier, inc=1, device_id=(target_of(i, m), partner), device_id_type=MESH)

    loop(0, outer, greet)
    loop(1, H, lambda k: pl.semaphore_signal(barrier, inc=1, device_id={"head": (j + k) % H}, device_id_type=MESH))

    local(mask_hbm, mask_v, in_sem.at[3])
    local(tseg_hbm, tseg_v, in_sem.at[4])
    local(pair_hbm, pair_v, in_sem.at[5])
    local(q_hbm, qg.at[0], in_sem.at[0])
    local(g_hbm, qg.at[1], in_sem.at[1])
    local(pair_hbm, pair_s, in_sem.at[6])
    local(sink_hbm, sink, in_sem.at[7])
    local(fseg_hbm, fseg_v, in_sem.at[8])
    local(kv_hbm, kv, in_sem.at[2])

    tag[...] = jnp.zeros(tag.shape, jnp.int32)
    wait(mask_v, in_sem.at[3])
    wait(tseg_v, in_sem.at[4])
    wait(pair_v, in_sem.at[5])
    tag[0:1, 0:text_rows] = tseg_v[...]
    tag[1:2, 0 : mask_v.shape[1]] = mask_v[...]
    column = jnp.broadcast_to(pair_v[...], (N, N)).T
    here = lax.broadcasted_iota(jnp.int32, (N, N), 1)
    source = lax.broadcasted_iota(jnp.int32, (N, N), 0)
    inv_v[...] = jnp.max(jnp.where(column == here, source, 0), axis=0, keepdims=True)
    local(inv_v, inv_s, inv_sem)
    wait(fseg_v, in_sem.at[8])
    for n in range(frames // BLOCK):
        fcol[n * BLOCK : (n + 1) * BLOCK, :] = jnp.broadcast_to(
            fseg_v[n : n + 1, :].astype(jnp.float32), (BLOCK, BLOCK)
        ).T
    wait(inv_v, inv_sem)
    wait(pair_s, in_sem.at[6])
    wait(sink, in_sem.at[7])
    wait(qg.at[0], in_sem.at[0])
    wait(qg.at[1], in_sem.at[1])
    wait(kv, in_sem.at[2])
    pl.semaphore_wait(barrier, N + H - 1)

    send(tag, tags_in.at[c], a1s, a1r, member(jnp.int32(tag_role)))
    for h in range(heads_here):

        def to_member(k):
            piece = (k + c) % pieces
            if N == 128:
                piece = (((c >> 4) + far(k // (pieces // 8))) & 7) + 8 * (k % (pieces // 8))
            slot = h * pieces + piece
            src = qg.at[piece // blocks, rows(piece % blocks), cols(h)]
            if (h + 1) * pieces <= N:
                send(src, arrived.at[c], t1s, t1r, member(slot))
            elif h * pieces >= N:
                send(src, arrived_more.at[c], t1s, m1r, member(slot - N))
            else:

                @pl.when(slot < N)
                def _():
                    send(src, arrived.at[c], t1s, t1r, member(slot))

                @pl.when(slot >= N)
                def _():
                    send(src, arrived_more.at[c], t1s, m1r, member(slot - N))

        loop(0, pieces, to_member)

    def place(s):
        return s & (N - 1)

    def pass_on(table, src, dst, target, ssem, rsem):
        def step(i):
            for m in range(N // outer):
                to = target_of(i, m)
                dst[to] = src[place(table[0, to])]
            for m in range(N // outer):
                to = target_of(i, m)
                send(dst.at[to], target, ssem, rsem, to)

        loop(0, outer, step)

    @pl.when(is_tag)
    def _():
        wait(tags_in, a1r)
        pass_on(inv_s, tags_in, tags_out, tag_here, a2s, a2r)

    def text_pass(slot, src, dst, rsem, ssem):
        head, piece = slot // pieces, slot % pieces
        wait(src, rsem)
        target = qr.at[piece // blocks, rows(piece % blocks), cols(head)]
        pass_on(inv_s, src, dst, target, ssem, t2r.at[head])

    @pl.when(is_text)
    def _():
        text_pass(role, arrived, ordered, t1r, t2s)

    if more:

        @pl.when(is_more)
        def _():
            text_pass(role + N, arrived_more, ordered_more, m1r, m2s)

    wait(tag_here, a2r)

    def attend(h):
        at = slice(h * DH, (h + 1) * DH)
        q = qr[0, :, at]
        g = qr[1, :, at]
        k = kv[0, :, at]
        v = kv[1, :, at]
        ids = tag_here[0:1, 0:text_rows].astype(jnp.float32)
        scores = _dot(k, q, 1, 1) * scale
        parts = []
        for n in range(frames // BLOCK):
            open_ = jnp.broadcast_to(tag_here[1:2, n : n + 1], ids.shape) == 1
            wanted = jnp.where(open_, ids, -1.0)
            at_n = slice(n * BLOCK, (n + 1) * BLOCK)
            allowed = fcol[at_n, 0:text_rows] == wanted
            parts.append(jnp.where(allowed, scores[at_n, :], -1e30))
        masked = jnp.concatenate(parts, axis=0)
        logit = jnp.full((1, text_rows), sink[0, h], jnp.float32)
        top = jnp.maximum(logit, jnp.max(masked, axis=0, keepdims=True))
        terms = jnp.exp(masked - top)
        total = jnp.exp(logit - top) + jnp.sum(terms, axis=0, keepdims=True)
        attention = terms * (1.0 / total)
        low = attention.astype(jnp.bfloat16)
        grad_attention = _dot(v, g, 1, 1)
        delta = jnp.sum(low.astype(jnp.float32) * grad_attention, axis=0, keepdims=True)
        grad_scores = (attention * (grad_attention - delta)).astype(jnp.bfloat16)
        dq[:, at] = (_dot(grad_scores, k, 0, 0) * scale).astype(jnp.bfloat16)

        def to_grad_member(n):
            block = (n + c) % blocks
            if N == 128:
                block = (((c >> 4) + far(n // (blocks // 8))) & 7) + 8 * (n % (blocks // 8))
            send(
                dq.at[rows(block), at], arrived_grad.at[c], g1s, g1r, member(first_grad + h * blocks + block)
            )

        loop(0, blocks, to_grad_member)
        low_kept[h] = low
        scores_kept[h] = grad_scores

    def share(h):
        at = slice(h * DH, (h + 1) * DH)
        dkv[0, :, at] = (_dot(scores_kept[h], qr[0, :, at], 1, 0) * scale).astype(jnp.bfloat16)
        dkv[1, :, at] = _dot(low_kept[h], qr[1, :, at], 1, 0).astype(jnp.bfloat16)
        out_cols = pl.ds(pl.multiple_of((j * heads_here + h) * DH, DH), DH)

        def part(x):
            return dkv.at[:, pl.ds(pl.multiple_of(x * frame_part, frame_part), frame_part), at]

        def to_peer(n):
            x = (j + n) % H
            pltpu.make_async_remote_copy(
                src_ref=part(x),
                dst_ref=dkv_out.at[:, :, out_cols],
                send_sem=ks,
                recv_sem=kr,
                device_id={"head": x},
                device_id_type=MESH,
            ).start()

        loop(1, H, to_peer)
        local(part(j), dkv_out.at[:, :, out_cols], kr)

    for h in range(heads_here):
        wait(qr.at[:, :, h * DH : (h + 1) * DH], t2r.at[h])
        attend(h)
        share(h)

    @pl.when(is_grad)
    def _():
        mine = role - first_grad
        wait(arrived_grad, g1r)
        pass_on(pair_s, arrived_grad, ordered_grad, dq_out.at[rows(mine % blocks), cols(mine // blocks)], g2s, g2r)

    wait(dq, g2r)
    wait(dkv, kr)
    wait(dkv.at[:, 0 : (H - 1) * frame_part, :], ks)

    wait(qg, t1s)
    wait(dq, g1s)
    wait(tag, a1s)

    @pl.when(is_tag)
    def _():
        wait(tags_out, a2s)

    @pl.when(is_text)
    def _():
        wait(ordered, t2s)

    if more:

        @pl.when(is_more)
        def _():
            wait(ordered_more, m2s)

    @pl.when(is_grad)
    def _():
        wait(ordered_grad, g2s)


def shards(text_query, grad_out, frame_kv, sink_logit, pairing, block_mask, text_seg, frame_seg):
    N = lax.axis_size("ctx")
    H = lax.axis_size("head")
    text_rows, width = text_query.shape
    frames = frame_kv.shape[1]
    bf = jnp.bfloat16
    dma = pltpu.SemaphoreType.DMA
    hbm = pl.BlockSpec(memory_space=pltpu.HBM)
    return pl.pallas_call(
        functools.partial(kernel, N, H),
        out_shape=(
            jax.ShapeDtypeStruct((text_rows, width), bf),
            jax.ShapeDtypeStruct((2, frames // H, width * H), bf),
        ),
        in_specs=[hbm] * 8,
        out_specs=(hbm, hbm),
        scratch_shapes=[
            pltpu.VMEM((2, text_rows, width), bf),
            pltpu.VMEM((2, frames, width), bf),
            pltpu.VMEM((N, TILE, DH), bf),
            pltpu.VMEM((N, TILE, DH), bf),
            pltpu.VMEM((N, TILE, DH), bf),
            pltpu.VMEM((N, TILE, DH), bf),
            pltpu.VMEM((N, TILE, DH), bf),
            pltpu.VMEM((N, TILE, DH), bf),
            pltpu.VMEM((2, text_rows, width), bf),
            pltpu.VMEM((2, frames, width), bf),
            pltpu.VMEM((text_rows, width), bf),
            pltpu.VMEM((2, 128), jnp.int32),
            pltpu.VMEM((N, 2, 128), jnp.int32),
            pltpu.VMEM((N, 2, 128), jnp.int32),
            pltpu.VMEM((2, 128), jnp.int32),
            pltpu.VMEM((width // DH, frames, text_rows), bf),
            pltpu.VMEM((width // DH, frames, text_rows), bf),
            pltpu.VMEM((frames, BLOCK), jnp.float32),
            pltpu.SMEM((1, width // DH), jnp.float32),
            pltpu.SMEM((1, N), jnp.int32),
            pltpu.VMEM((1, N), jnp.int32),
            pltpu.VMEM((1, frames // BLOCK), jnp.int32),
            pltpu.VMEM((1, text_rows), jnp.int32),
            pltpu.VMEM((frames // BLOCK, BLOCK), jnp.int32),
            pltpu.VMEM((1, N), jnp.int32),
            pltpu.SMEM((1, N), jnp.int32),
            dma((9,)),
            dma,
            dma, dma, dma, dma((width // DH,)), dma, dma, dma, dma, dma, dma, dma, dma, dma, dma, dma, dma,
        ],
        compiler_params=pltpu.CompilerParams(
            collective_id=0, has_side_effects=True, vmem_limit_bytes=40 * 1024 * 1024
        ),
        name="paired_attention_grads",
    )(
        *(
            pltpu.with_memory_space_constraint(x, pltpu.HBM)
            for x in (
                text_query,
                grad_out,
                frame_kv,
                sink_logit.reshape(1, width // DH),
                pairing.reshape(1, N),
                block_mask,
                text_seg.reshape(1, text_rows),
                frame_seg.reshape(frames // BLOCK, BLOCK),
            )
        )
    )


def solution(mesh):
    in_specs = (
        P("ctx", "head"),
        P("ctx", "head"),
        P(None, "ctx", "head"),
        P("head"),
        P(),
        P("ctx", None),
        P("ctx"),
        P("ctx"),
    )
    out_specs = (P("ctx", "head"), P(None, ("ctx", "head"), None))
    return jax.shard_map(shards, mesh=mesh, in_specs=in_specs, out_specs=out_specs, check_vma=False)
```

```python
import functools

import jax
import jax.numpy as jnp
from jax import lax
from jax.experimental import pallas as pl
from jax.experimental.pallas import tpu as pltpu
from jax.sharding import PartitionSpec as P

DH = 128
BLOCK = 128
TILE = 8
MESH = pl.DeviceIdType.MESH


def _dot(a, b, ca, cb):
    return lax.dot_general(a, b, (((ca,), (cb,)), ((), ())), preferred_element_type=jnp.float32)


def kernel(
    N, H,
    q_hbm, g_hbm, kv_hbm, sink_hbm, pair_hbm, mask_hbm, tseg_hbm, fseg_hbm,
    dq_out, dkv_out,
    qg, kv, arrived, ordered, arrived_more, ordered_more, arrived_grad, ordered_grad, qr, dkv, dq, tag, tags_in, tags_out, tag_here,
    low_kept, scores_kept, fcol, sink, pair_s, pair_v, mask_v, tseg_v, fseg_v, inv_v, inv_s,
    in_sem, inv_sem,
    t1s, t1r, t2s, t2r, m1r, m2s, g1s, g1r, g2s, g2r, ks, kr, a1s, a1r, a2s, a2r,
):
    scale = DH ** (-0.5)
    c = lax.axis_index("ctx")
    j = lax.axis_index("head")
    text_rows = q_hbm.shape[0]
    heads_here = q_hbm.shape[1] // DH
    frames = kv_hbm.shape[1]
    frame_part = frames // H
    blocks = text_rows // TILE
    pieces = 2 * blocks
    text_roles = heads_here * pieces
    grad_roles = heads_here * blocks
    more = max(text_roles - N, 0)
    first_grad = N - grad_roles
    tag_role = N - 1
    core = j % 2 if N == 128 else 0
    partner = (j + H // 2) % H

    def member(role):
        if N != 128:
            return jnp.where(core == 1, N - 1 - role, role)
        y, x, r = role & 7, (role >> 3) & 1, role >> 4
        r = jnp.where(core == 1, 7 - r, r)
        turned = ((r & 1) << 2) | (r & 2) | (r >> 2)
        return (y << 4) | (x << 3) | ((3 * y + 4 * x + turned) & 7)

    def role_of(device):
        if N != 128:
            return jnp.where(core == 1, N - 1 - device, device)
        y, x, z = device >> 4, (device >> 3) & 1, device & 7
        turned = (z + 32 - 3 * y - 4 * x) & 7
        r = ((turned & 1) << 2) | (turned & 2) | (turned >> 2)
        r = jnp.where(core == 1, 7 - r, r)
        return (r << 4) | (x << 3) | y

    role = role_of(c)
    is_text = role < text_roles
    is_grad = role >= first_grad
    is_tag = role == tag_role
    is_more = role < more

    outer = 8 if N == 128 else 1

    def far(i):
        return 4 + (1 - 2 * (i % 2)) * ((i + 1) // 2)

    def target_of(i, m):
        if N != 128:
            return (c + m) % N
        y, x, z = c >> 4, (c >> 3) & 1, c & 7
        return (((y + far(m // 2)) & 7) << 4) | (((x + m % 2) & 1) << 3) | ((z + far(i)) & 7)

    def cols(h):
        return pl.ds(pl.multiple_of(h * DH, DH), DH)

    def rows(x):
        return pl.ds(pl.multiple_of(x * TILE, TILE), TILE)

    def send(src, dst, ssem, rsem, ctx):
        pltpu.make_async_remote_copy(
            src_ref=src, dst_ref=dst, send_sem=ssem, recv_sem=rsem, device_id=(ctx, partner), device_id_type=MESH
        ).start()

    def local(src, dst, sem):
        pltpu.make_async_copy(src, dst, sem).start()

    def wait(ref, sem):
        pltpu.make_async_copy(ref, ref, sem).wait()

    def loop(low, high, body):
        def step(k, carry):
            body(k)
            return carry

        lax.fori_loop(low, high, step, 0)

    barrier = pltpu.get_barrier_semaphore()

    def greet(i):
        for m in range(N // outer):
            pl.semaphore_signal(barrier, inc=1, device_id=(target_of(i, m), partner), device_id_type=MESH)

    loop(0, outer, greet)
    loop(1, H, lambda k: pl.semaphore_signal(barrier, inc=1, device_id={"head": (j + k) % H}, device_id_type=MESH))

    local(mask_hbm, mask_v, in_sem.at[3])
    local(tseg_hbm, tseg_v, in_sem.at[4])
    local(pair_hbm, pair_v, in_sem.at[5])
    local(q_hbm, qg.at[0], in_sem.at[0])
    local(g_hbm, qg.at[1], in_sem.at[1])
    local(pair_hbm, pair_s, in_sem.at[6])
    local(sink_hbm, sink, in_sem.at[7])
    local(fseg_hbm, fseg_v, in_sem.at[8])
    local(kv_hbm, kv, in_sem.at[2])

    tag[...] = jnp.zeros(tag.shape, jnp.int32)
    wait(mask_v, in_sem.at[3])
    wait(tseg_v, in_sem.at[4])
    wait(pair_v, in_sem.at[5])
    tag[0:1, 0:text_rows] = tseg_v[...]
    tag[1:2, 0 : mask_v.shape[1]] = mask_v[...]
    column = jnp.broadcast_to(pair_v[...], (N, N)).T
    here = lax.broadcasted_iota(jnp.int32, (N, N), 1)
    source = lax.broadcasted_iota(jnp.int32, (N, N), 0)
    inv_v[...] = jnp.max(jnp.where(column == here, source, 0), axis=0, keepdims=True)
    local(inv_v, inv_s, inv_sem)
    wait(fseg_v, in_sem.at[8])
    for n in range(frames // BLOCK):
        fcol[n * BLOCK : (n + 1) * BLOCK, :] = jnp.broadcast_to(
            fseg_v[n : n + 1, :].astype(jnp.float32), (BLOCK, BLOCK)
        ).T
    wait(inv_v, inv_sem)
    wait(pair_s, in_sem.at[6])
    wait(sink, in_sem.at[7])
    wait(qg.at[0], in_sem.at[0])
    wait(qg.at[1], in_sem.at[1])
    wait(kv, in_sem.at[2])
    pl.semaphore_wait(barrier, N + H - 1)

    send(tag, tags_in.at[c], a1s, a1r, member(jnp.int32(tag_role)))
    for h in range(heads_here):

        def to_member(k):
            piece = (k + c) % pieces
            if N == 128:
                piece = (((c >> 4) + far(k // (pieces // 8))) & 7) + 8 * (k % (pieces // 8))
            slot = h * pieces + piece
            src = qg.at[piece // blocks, rows(piece % blocks), cols(h)]
            if (h + 1) * pieces <= N:
                send(src, arrived.at[c], t1s, t1r, member(slot))
            elif h * pieces >= N:
                send(src, arrived_more.at[c], t1s, m1r, member(slot - N))
            else:

                @pl.when(slot < N)
                def _():
                    send(src, arrived.at[c], t1s, t1r, member(slot))

                @pl.when(slot >= N)
                def _():
                    send(src, arrived_more.at[c], t1s, m1r, member(slot - N))

        loop(0, pieces, to_member)

    def place(s):
        return s & (N - 1)

    def pass_on(table, src, dst, target, ssem, rsem):
        def step(i):
            for m in range(N // outer):
                to = target_of(i, m)
                dst[to] = src[place(table[0, to])]
            for m in range(N // outer):
                to = target_of(i, m)
                send(dst.at[to], target, ssem, rsem, to)

        loop(0, outer, step)

    @pl.when(is_tag)
    def _():
        wait(tags_in, a1r)
        pass_on(inv_s, tags_in, tags_out, tag_here, a2s, a2r)

    def text_pass(slot, src, dst, rsem, ssem):
        head, piece = slot // pieces, slot % pieces
        wait(src, rsem)
        target = qr.at[piece // blocks, rows(piece % blocks), cols(head)]
        pass_on(inv_s, src, dst, target, ssem, t2r.at[head])

    @pl.when(is_text)
    def _():
        text_pass(role, arrived, ordered, t1r, t2s)

    if more:

        @pl.when(is_more)
        def _():
            text_pass(role + N, arrived_more, ordered_more, m1r, m2s)

    wait(tag_here, a2r)

    def attend(h):
        at = slice(h * DH, (h + 1) * DH)
        q = qr[0, :, at]
        g = qr[1, :, at]
        k = kv[0, :, at]
        v = kv[1, :, at]
        ids = tag_here[0:1, 0:text_rows].astype(jnp.float32)
        scores = _dot(k, q, 1, 1) * scale
        parts = []
        for n in range(frames // BLOCK):
            open_ = jnp.broadcast_to(tag_here[1:2, n : n + 1], ids.shape) == 1
            wanted = jnp.where(open_, ids, -1.0)
            at_n = slice(n * BLOCK, (n + 1) * BLOCK)
            allowed = fcol[at_n, 0:text_rows] == wanted
            parts.append(jnp.where(allowed, scores[at_n, :], -1e30))
        masked = jnp.concatenate(parts, axis=0)
        logit = jnp.full((1, text_rows), sink[0, h], jnp.float32)
        top = jnp.maximum(logit, jnp.max(masked, axis=0, keepdims=True))
        terms = jnp.exp(masked - top)
        total = jnp.exp(logit - top) + jnp.sum(terms, axis=0, keepdims=True)
        attention = terms * (1.0 / total)
        low = attention.astype(jnp.bfloat16)
        grad_attention = _dot(v, g, 1, 1)
        delta = jnp.sum(low.astype(jnp.float32) * grad_attention, axis=0, keepdims=True)
        grad_scores = (attention * (grad_attention - delta)).astype(jnp.bfloat16)
        dq[:, at] = (_dot(grad_scores, k, 0, 0) * scale).astype(jnp.bfloat16)

        def to_grad_member(n):
            block = (n + c) % blocks
            if N == 128:
                block = (((c >> 4) + far(n // (blocks // 8))) & 7) + 8 * (n % (blocks // 8))
            send(
                dq.at[rows(block), at], arrived_grad.at[c], g1s, g1r, member(first_grad + h * blocks + block)
            )

        loop(0, blocks, to_grad_member)
        low_kept[h] = low
        scores_kept[h] = grad_scores

    def share(h):
        at = slice(h * DH, (h + 1) * DH)
        dkv[0, :, at] = (_dot(scores_kept[h], qr[0, :, at], 1, 0) * scale).astype(jnp.bfloat16)
        dkv[1, :, at] = _dot(low_kept[h], qr[1, :, at], 1, 0).astype(jnp.bfloat16)
        out_cols = pl.ds(pl.multiple_of((j * heads_here + h) * DH, DH), DH)

        def part(x):
            return dkv.at[:, pl.ds(pl.multiple_of(x * frame_part, frame_part), frame_part), at]

        def to_peer(n):
            x = (j + n) % H
            pltpu.make_async_remote_copy(
                src_ref=part(x),
                dst_ref=dkv_out.at[:, :, out_cols],
                send_sem=ks,
                recv_sem=kr,
                device_id={"head": x},
                device_id_type=MESH,
            ).start()

        loop(1, H, to_peer)
        local(part(j), dkv_out.at[:, :, out_cols], kr)

    for h in range(heads_here):
        wait(qr.at[:, :, h * DH : (h + 1) * DH], t2r.at[h])
        attend(h)
        share(h)

    @pl.when(is_grad)
    def _():
        mine = role - first_grad
        wait(arrived_grad, g1r)
        pass_on(pair_s, arrived_grad, ordered_grad, dq_out.at[rows(mine % blocks), cols(mine // blocks)], g2s, g2r)

    wait(dq, g2r)
    wait(dkv, kr)
    wait(dkv.at[:, 0 : (H - 1) * frame_part, :], ks)

    wait(qg, t1s)
    wait(dq, g1s)
    wait(tag, a1s)

    @pl.when(is_tag)
    def _():
        wait(tags_out, a2s)

    @pl.when(is_text)
    def _():
        wait(ordered, t2s)

    if more:

        @pl.when(is_more)
        def _():
            wait(ordered_more, m2s)

    @pl.when(is_grad)
    def _():
        wait(ordered_grad, g2s)


def shards(text_query, grad_out, frame_kv, sink_logit, pairing, block_mask, text_seg, frame_seg):
    N = lax.axis_size("ctx")
    H = lax.axis_size("head")
    text_rows, width = text_query.shape
    frames = frame_kv.shape[1]
    bf = jnp.bfloat16
    dma = pltpu.SemaphoreType.DMA
    hbm = pl.BlockSpec(memory_space=pltpu.HBM)
    return pl.pallas_call(
        functools.partial(kernel, N, H),
        out_shape=(
            jax.ShapeDtypeStruct((text_rows, width), bf),
            jax.ShapeDtypeStruct((2, frames // H, width * H), bf),
        ),
        in_specs=[hbm] * 8,
        out_specs=(hbm, hbm),
        scratch_shapes=[
            pltpu.VMEM((2, text_rows, width), bf),
            pltpu.VMEM((2, frames, width), bf),
            pltpu.VMEM((N, TILE, DH), bf),
            pltpu.VMEM((N, TILE, DH), bf),
            pltpu.VMEM((N, TILE, DH), bf),
            pltpu.VMEM((N, TILE, DH), bf),
            pltpu.VMEM((N, TILE, DH), bf),
            pltpu.VMEM((N, TILE, DH), bf),
            pltpu.VMEM((2, text_rows, width), bf),
            pltpu.VMEM((2, frames, width), bf),
            pltpu.VMEM((text_rows, width), bf),
            pltpu.VMEM((2, 128), jnp.int32),
            pltpu.VMEM((N, 2, 128), jnp.int32),
            pltpu.VMEM((N, 2, 128), jnp.int32),
            pltpu.VMEM((2, 128), jnp.int32),
            pltpu.VMEM((width // DH, frames, text_rows), bf),
            pltpu.VMEM((width // DH, frames, text_rows), bf),
            pltpu.VMEM((frames, BLOCK), jnp.float32),
            pltpu.SMEM((1, width // DH), jnp.float32),
            pltpu.SMEM((1, N), jnp.int32),
            pltpu.VMEM((1, N), jnp.int32),
            pltpu.VMEM((1, frames // BLOCK), jnp.int32),
            pltpu.VMEM((1, text_rows), jnp.int32),
            pltpu.VMEM((frames // BLOCK, BLOCK), jnp.int32),
            pltpu.VMEM((1, N), jnp.int32),
            pltpu.SMEM((1, N), jnp.int32),
            dma((9,)),
            dma,
            dma, dma, dma, dma((width // DH,)), dma, dma, dma, dma, dma, dma, dma, dma, dma, dma, dma, dma,
        ],
        compiler_params=pltpu.CompilerParams(
            collective_id=0, has_side_effects=True, vmem_limit_bytes=40 * 1024 * 1024
        ),
        name="paired_attention_grads",
    )(
        *(
            pltpu.with_memory_space_constraint(x, pltpu.HBM)
            for x in (
                text_query,
                grad_out,
                frame_kv,
                sink_logit.reshape(1, width // DH),
                pairing.reshape(1, N),
                block_mask,
                text_seg.reshape(1, text_rows),
                frame_seg.reshape(frames // BLOCK, BLOCK),
            )
        )
    )


def solution(mesh):
    in_specs = (
        P("ctx", "head"),
        P("ctx", "head"),
        P(None, "ctx", "head"),
        P("head"),
        P(),
        P("ctx", None),
        P("ctx"),
        P("ctx"),
    )
    out_specs = (P("ctx", "head"), P(None, ("ctx", "head"), None))
    return jax.shard_map(shards, mesh=mesh, in_specs=in_specs, out_specs=out_specs, check_vma=False)
```
